32 devices in a mesh: ka: 8 (over z, y), col: 4 (over x, core).
Axes of the slice: x: 2, y: 2, z: 4, core: 2. Of those that a mesh axis runs over, the one named last changes fastest.
Arguments:
- hamiltonian: bfloat16 [1024, 2, 9216], P(('ka', 'col')), may hold values from -0.1875 to 0.1875
- eigvecs: bfloat16 [512, 2, 96, 96], P('ka'), may hold values from -0.625 to 0.625
- spin: bfloat16 [2, 96, 96], replicated, may hold values from -0.059814453 to 0.059814453
- k_indices: int32 [512, 3], P('ka'), may hold values from 0 to 63
- r_vectors: int32 [1024, 3], replicated, may hold values from -5 to 5, as said below
- degeneracy: int32 [1024], replicated, may hold values from 1 to 4
- fermi_level: float32 [1], replicated, may hold values from -0.5 to 0.5
Outputs:
- band_curvature: float32 [9, 96, 512], P(None, None, ('ka', 'col'))
- conductivity: float32 [9, 96], replicated
The draws below stay inside these ranges and needn't reach their ends.
Inputs may be any that keep to these rules, and one draw needn't show every extreme that they name: `r_vectors`: the 1024 lattice vectors are all distinct.
All inputs are finite; a program needn't handle non-finite values.
Results may differ from the reference program's by a relative error of at most 0.0085.
The reference program's roundings to bfloat16 on the way count: a program that leaves them out, or rounds other values in their place, can miss the bound.
Values may be sent and summed in bfloat16 or wider, within the bound.
A program may use at most 128 MiB of HBM per device.

```python
import math
import jax
import jax.numpy as jnp
from jax import lax

WF = 96
NR = 1024
K_DEV = 64
GRID = 64
NK = 512


def draw_r_vectors(key, part):
    codes = jax.random.permutation(jax.random.fold_in(key, 17), jnp.arange(1331, dtype=jnp.int32))[:NR]
    first = codes // 121
    second = codes // 11 % 11
    third = codes % 11
    return (jnp.stack([first, second, third], axis=1) - 5).astype(jnp.int32)


def place_ends(entries, key, least, top_value):
    longest = entries.shape.index(max(entries.shape))
    spots = []
    for shift in (0, 1):
        where = [jax.random.randint(jax.random.fold_in(key, axis), (), 0, length) for axis, length in enumerate(entries.shape)]
        where[longest] = (where[longest] + shift) % entries.shape[longest]
        spots.append(tuple(where))
    return entries.at[spots[0]].set(least).at[spots[1]].set(top_value)


def block_levels(stream_key, extent, split, least, largest):
    def one(axis_at, parts):
        draws = jax.random.uniform(jax.random.fold_in(jax.random.fold_in(stream_key, 6), axis_at), (parts,), jnp.float32, least / len(split), largest / len(split))
        return jnp.repeat(jnp.exp(draws), extent[axis_at] // parts).reshape((-1,) + (1,) * (len(extent) - axis_at - 1))

    loudness = one(*split[0])
    for cut in split[1:]:
        loudness = loudness * one(*cut)
    return loudness


def bell_draw(rng, extent, scale, bound, cuts=(), kind=jnp.bfloat16):
    entries = scale * jax.random.normal(rng, extent, jnp.float32)
    if cuts:
        entries = entries * block_levels(rng, extent, cuts, -0.22, 0.18)
    return jnp.clip(entries, -bound, bound).astype(kind)


def setup_inputs(seed: int = 0) -> dict:
    keys = jax.random.split(jax.random.key(seed), 8)
    hamiltonian = bell_draw(keys[0], (NR, 2, WF * WF), NR ** -0.5, 0.1875, ((0, 32),))
    eigvecs = bell_draw(keys[1], (NK, 2, WF, WF), WF ** -0.5, 0.625, ((0, 8),))
    spin = bell_draw(keys[2], (2, WF, WF), 0.01, 0.059814453)
    k_indices = place_ends(jax.random.randint(keys[3], (NK, 3), 0, GRID), jax.random.fold_in(keys[3], 1), 0, GRID - 1).astype(jnp.int32)
    r_vectors = draw_r_vectors(jax.random.fold_in(keys[7], 71), 0)
    degeneracy = place_ends(jax.random.randint(keys[5], (NR,), 1, 5), jax.random.fold_in(keys[5], 1), 1, 4).astype(jnp.int32)
    fermi_level = jnp.clip(jax.random.uniform(keys[6], (1,), jnp.float32, -0.5, 0.5), -0.5, 0.5)
    return {"hamiltonian": hamiltonian, "eigvecs": eigvecs, "spin": spin, "k_indices": k_indices, "r_vectors": r_vectors, "degeneracy": degeneracy, "fermi_level": fermi_level}


two_pi = 2.0 * math.pi
broadening = 0.5
smearing = 0.1

def phase_table(kpoints, lattice, degrees):
    lattice_dot = jnp.mod(lax.optimization_barrier(jnp.sum(kpoints[:, None, :] * lattice[None, :, :], axis=-1)), GRID)
    angles = lattice_dot.astype(jnp.float32) * (two_pi / GRID)
    cosine = jnp.cos(angles)
    sine_part = jnp.sin(angles)
    inverse = 1.0 / degrees.astype(jnp.float32)
    coords = lattice.astype(jnp.float32) * inverse[:, None]
    real_part = jnp.stack([cosine * inverse, -sine_part * coords[:, 0], -sine_part * coords[:, 1], -sine_part * coords[:, 2]], axis=1)
    imag_part = jnp.stack([sine_part * inverse, cosine * coords[:, 0], cosine * coords[:, 1], cosine * coords[:, 2]], axis=1)
    top_rows = jnp.stack([real_part, -imag_part], axis=-1)
    low_rows = jnp.stack([imag_part, real_part], axis=-1)
    return jnp.stack([top_rows, low_rows], axis=2)

def rotate(operators, vectors):
    ops_re = operators[:, :, 0].astype(jnp.float32)
    ops_im = operators[:, :, 1].astype(jnp.float32)
    vec_re = vectors[:, 0].astype(jnp.float32)
    vec_im = vectors[:, 1].astype(jnp.float32)
    half_re = jnp.einsum('kcij,kjm->kcim', ops_re, vec_re) - jnp.einsum('kcij,kjm->kcim', ops_im, vec_im)
    half_im = jnp.einsum('kcij,kjm->kcim', ops_re, vec_im) + jnp.einsum('kcij,kjm->kcim', ops_im, vec_re)
    half_re = lax.optimization_barrier(half_re.astype(jnp.bfloat16)).astype(jnp.float32)
    half_im = lax.optimization_barrier(half_im.astype(jnp.bfloat16)).astype(jnp.float32)
    full_re = jnp.einsum('kjn,kcjm->kcnm', vec_re, half_re) + jnp.einsum('kjn,kcjm->kcnm', vec_im, half_im)
    full_im = jnp.einsum('kjn,kcjm->kcnm', vec_re, half_im) - jnp.einsum('kjn,kcjm->kcnm', vec_im, half_re)
    sym_re = (full_re + jnp.swapaxes(full_re, -1, -2)) * 0.5
    sym_im = (full_im - jnp.swapaxes(full_im, -1, -2)) * 0.5
    return jnp.stack([sym_re, sym_im], axis=2).astype(jnp.bfloat16)

def kubo(bloch_ops, spin_bloch, fermi_level):
    energy = jnp.diagonal(bloch_ops[:, 0, 0].astype(jnp.float32), axis1=-2, axis2=-1)
    velo_re = bloch_ops[:, 1:, 0].astype(jnp.float32)
    velo_im = bloch_ops[:, 1:, 1].astype(jnp.float32)
    spin_re = spin_bloch[:, 0].astype(jnp.float32)
    spin_im = spin_bloch[:, 1].astype(jnp.float32)
    prod_re = jnp.einsum('kij,kajm->kaim', spin_re, velo_re) - jnp.einsum('kij,kajm->kaim', spin_im, velo_im)
    prod_im = jnp.einsum('kij,kajm->kaim', spin_re, velo_im) + jnp.einsum('kij,kajm->kaim', spin_im, velo_re)
    cur_re = (prod_re + jnp.swapaxes(prod_re, -1, -2)) * 0.5
    cur_im = (prod_im - jnp.swapaxes(prod_im, -1, -2)) * 0.5
    energy_gap = energy[:, :, None] - energy[:, None, :]
    weight = 1.0 / (energy_gap * energy_gap + broadening * broadening)
    curvature = -2.0 * (jnp.einsum('kanm,kbmn,knm->kabn', cur_re, velo_im, weight) + jnp.einsum('kanm,kbmn,knm->kabn', cur_im, velo_re, weight))
    occupation = 1.0 / (1.0 + jnp.exp((energy - fermi_level[0]) / smearing))
    weighted = jnp.einsum('kn,kabn->abn', occupation, curvature)
    return (curvature, weighted)

def reference(hamiltonian, eigvecs, spin, k_indices, r_vectors, degeneracy, fermi_level):
    block_count = NK // K_DEV
    hopping = hamiltonian.reshape(NR * 2, WF * WF)
    spin_wide = spin.astype(jnp.float32)
    spin_sym = jnp.stack([(spin_wide[0] + spin_wide[0].T) * 0.5, (spin_wide[1] - spin_wide[1].T) * 0.5]).astype(jnp.bfloat16)

    def one_block(block_index):
        kpoints = lax.dynamic_slice_in_dim(k_indices, block_index * K_DEV, K_DEV, 0)
        vectors = lax.dynamic_slice_in_dim(eigvecs, block_index * K_DEV, K_DEV, 0)
        phases = phase_table(kpoints, r_vectors, degeneracy).reshape(K_DEV * 8, NR * 2).astype(jnp.bfloat16)
        summed = jnp.dot(phases, hopping, preferred_element_type=jnp.float32)
        interpolated = summed.reshape(K_DEV, 4, 2, WF, WF).astype(jnp.bfloat16)
        bloch_ops = rotate(interpolated, vectors)
        spin_ops = jnp.broadcast_to(spin_sym[None, None], (K_DEV, 1, 2, WF, WF))
        spin_bloch = rotate(spin_ops, vectors)[:, 0]
        return kubo(bloch_ops, spin_bloch, fermi_level)
    curvature, weighted = lax.map(one_block, jnp.arange(block_count, dtype=jnp.int32))
    curvature = curvature.reshape(NK, 3, 3, WF)
    band_curvature = jnp.transpose(curvature, (1, 2, 3, 0)).reshape(9, WF, NK)
    conductivity = (lax.optimization_barrier(jnp.sum(weighted, axis=0)) / math.sqrt(NK)).reshape(9, WF)
    return (band_curvature, conductivity)
```

```python
import functools
import math

import jax
import jax.numpy as jnp
from jax import lax
from jax.experimental import pallas as pl
from jax.experimental.pallas import tpu as pltpu
from jax.sharding import PartitionSpec as P

GRID = 64
broadening = 0.5
smearing = 0.1
LO = 2
PAD = 128
MESH = pl.DeviceIdType.MESH
f32 = jnp.float32
bf16 = jnp.bfloat16


def half_wave(t):
    v = jnp.abs(t - GRID / 2) - GRID / 4
    y = v * (2.0 * math.pi / GRID)
    z = y * y
    p = jnp.full_like(z, 1.0 / 6227020800.0)
    for den in (-39916800.0, 362880.0, -5040.0, 120.0, -6.0):
        p = p * z + 1.0 / den
    return y * (p * z) + y


def kernel(
    cfg,
    h_ref,
    ev_ref,
    spin_ref,
    kf_ref,
    table_ref,
    fermi_ref,
    curv_ref,
    total_ref,
    kall,
    gath,
    phase,
    outs,
    xin,
    y_re,
    y_im,
    upad,
    amat,
    acc,
    red1,
    red2,
    loc_sem,
    k_sem,
    sa,
    ra,
    sl,
    rl,
    so,
    ro,
    s1,
    r1,
    s2,
    r2,
):
    WF, L, ncol, rows, nch, cw, kdev, quarter, total_points = cfg
    E = LO * ncol
    ka = lax.axis_index("ka")
    col = lax.axis_index("col")
    hi = ka // LO
    lo = ka % LO
    me = lo * ncol + col

    def peer(step):
        e = lax.rem(me + step, E)
        return e, (hi * LO + e // ncol, lax.rem(e, ncol))

    def line(h):
        return (h * LO + lo, col)

    barrier = pltpu.get_barrier_semaphore()
    for step in range(1, E):
        pl.semaphore_signal(barrier, inc=1, device_id=peer(step)[1], device_id_type=MESH)
    for step in range(1, L):
        pl.semaphore_signal(
            barrier, inc=1, device_id=line(lax.rem(hi + step, L)), device_id_type=MESH
        )
    pl.semaphore_wait(barrier, E - 1 + L - 1)

    src_me = hi * E + me

    def plane_copy(n, step):
        e, dev = peer(step)
        return pltpu.make_async_remote_copy(
            src_ref=h_ref.at[:, pl.ds(pl.multiple_of(e * (nch * cw) + n * cw, 128), cw)],
            dst_ref=gath.at[n, src_me],
            send_sem=sa.at[n, step],
            recv_sem=ra.at[n, step],
            device_id=dev,
            device_id_type=MESH,
        )

    def plane_local(n):
        return pltpu.make_async_copy(
            h_ref.at[:, pl.ds(pl.multiple_of(me * (nch * cw) + n * cw, 128), cw)],
            gath.at[n, src_me],
            loc_sem.at[n],
        )

    def line_copy(n, unit, up):
        tgt = hi + 1 if up else hi - 1
        return pltpu.make_async_remote_copy(
            src_ref=gath.at[n, pl.ds(unit * E, E)],
            dst_ref=gath.at[n, pl.ds(unit * E, E)],
            send_sem=sl.at[n, unit, 0 if up else 1],
            recv_sem=rl.at[n, unit],
            device_id=line(tgt),
            device_id_type=MESH,
        )

    k_copy = pltpu.make_async_remote_copy(
        src_ref=kf_ref,
        dst_ref=kall.at[lo],
        send_sem=k_sem.at[0],
        recv_sem=k_sem.at[1],
        device_id=(hi * LO + (1 - lo), col),
        device_id_type=MESH,
    )
    k_copy.start()
    k_local = pltpu.make_async_copy(kf_ref, kall.at[lo], k_sem.at[2])
    k_local.start()
    for n in range(nch):
        plane_local(n).start()
        for step in range(1, E):
            plane_copy(n, step).start()

    def own_units(n):
        plane_local(n).wait()
        for step in range(1, E):
            plane_copy(n, step).wait_recv()

        @pl.when(hi + 1 < L)
        def _():
            line_copy(n, hi, True).start()

        @pl.when(hi > 0)
        def _():
            line_copy(n, hi, False).start()

    def forward(n, d):
        @pl.when(hi - d >= 0)
        def _():
            line_copy(n, hi - d, True).wait_recv()

            @pl.when(hi + 1 < L)
            def _():
                line_copy(n, hi - d, True).start()

        @pl.when(hi + d < L)
        def _():
            line_copy(n, hi + d, False).wait_recv()

            @pl.when(hi > 0)
            def _():
                line_copy(n, hi + d, False).start()

    own_units(0)
    if nch > 1:
        own_units(1)

    k_copy.wait()
    k_local.wait()
    y_re[...] = jnp.zeros_like(y_re)
    y_im[...] = jnp.zeros_like(y_im)
    upad[...] = jnp.zeros_like(upad)
    amat[...] = jnp.zeros_like(amat)
    acc[...] = jnp.zeros_like(acc)
    sre = spin_ref[0].astype(f32)
    sim = spin_ref[1].astype(f32)
    upad[0, 0:WF, 0:WF] = sre
    upad[1, 0:WF, 0:WF] = sim
    sre = upad[0]
    sim = upad[1]
    amat[4 * PAD : 5 * PAD, 0:PAD] = ((sre + sre.T) * 0.5).astype(bf16)
    amat[4 * PAD : 5 * PAD, PAD : 2 * PAD] = ((sim - sim.T) * 0.5).astype(bf16)

    lanes = table_ref.shape[1]
    lw = 512 if lanes % 512 == 0 else 128
    per_lo = kdev // quarter

    def phase_body(idx, carry):
        dest = idx // (lanes // lw)
        off = pl.multiple_of(lax.rem(idx, lanes // lw) * lw, 128)
        kk = kall[dest // per_lo, pl.ds(pl.multiple_of(lax.rem(dest, per_lo) * quarter, 8), quarter), :]
        tab = table_ref[:, pl.ds(off, lw)]
        dot = (
            kk[:, 0:1] * tab[0:1, :]
            + kk[:, 1:2] * tab[1:2, :]
            + kk[:, 2:3] * tab[2:3, :]
            + tab[3:4, :]
        )
        t = dot - GRID * jnp.floor(dot * (1.0 / GRID))
        tq = t + (3 * GRID // 4)
        tq = jnp.where(tq >= GRID, tq - GRID, tq)
        cosine = half_wave(t)
        sine = half_wave(tq)
        base = pl.multiple_of(dest * (8 * quarter), 16)
        for c in range(4):
            if c == 0:
                top = cosine * tab[4:5, :]
                low = sine * tab[4:5, :]
            else:
                top = -sine * tab[4 + c : 5 + c, :]
                low = cosine * tab[4 + c : 5 + c, :]
            phase[pl.ds(base + c * quarter, quarter), pl.ds(off, lw)] = top.astype(bf16)
            phase[pl.ds(base + (4 + c) * quarter, quarter), pl.ds(off, lw)] = low.astype(bf16)
        return carry

    lax.fori_loop(0, E * (lanes // lw), phase_body, 0)

    def out_copy(n, step):
        e, dev = peer(step)
        return pltpu.make_async_remote_copy(
            src_ref=outs.at[n, e],
            dst_ref=xin.at[n, me],
            send_sem=so.at[n, step],
            recv_sem=ro.at[n, step],
            device_id=dev,
            device_id_type=MESH,
        )

    blk = 8 * quarter

    for n in range(nch):
        for d in range(1, L):
            forward(n, d)
            if d == 1 and n + 2 < nch:
                own_units(n + 2)

        def mm(step, carry, n=n):
            e = lax.rem(me + step, E)
            rhs = gath[n].reshape(lanes, cw)
            res = jnp.dot(
                phase[pl.ds(pl.multiple_of(e * blk, 16), blk), :],
                rhs,
                preferred_element_type=f32,
            ).astype(bf16)

            @pl.when(step < E)
            def _():
                outs[n, e] = res
                out_copy(n, step).start()

            @pl.when(step == E)
            def _():
                xin[n, me] = res

            return carry

        lax.fori_loop(1, E + 1, mm, 0)

    half_rows = 4 * quarter
    per = cw // WF
    for n in range(nch):
        for step in range(1, E):
            out_copy(n, step).wait_recv()

        def unflat(e, carry, n=n):
            x = xin[n, e].astype(f32)
            for q in range(per):
                i = e * (nch * per) + n * per + q
                at = pl.ds(pl.multiple_of(i * half_rows, 8), half_rows)
                y_re[at, 0:WF] = x[0:half_rows, q * WF : (q + 1) * WF]
                y_im[at, 0:WF] = x[half_rows:, q * WF : (q + 1) * WF]
            return carry

        lax.fori_loop(0, E, unflat, 0)

    row = lax.broadcasted_iota(jnp.int32, (PAD, PAD), 0)
    lane = lax.broadcasted_iota(jnp.int32, (PAD, PAD), 1)
    eye = row == lane
    fermi = fermi_ref[0]
    NT = (((1,), (1,)), ((), ()))

    def one_k(k, carry):
        upad[0, 0:WF, 0:WF] = ev_ref[col * quarter + k, 0].astype(f32)
        upad[1, 0:WF, 0:WF] = ev_ref[col * quarter + k, 1].astype(f32)
        ur = upad[0]
        ui = upad[1]
        urt = ur.T.astype(bf16)
        uit = ui.T.astype(bf16)
        ur = ur.astype(bf16)
        ui = ui.astype(bf16)
        cat = jnp.concatenate
        first = cat([cat([urt, -uit], 1), cat([uit, urt], 1)], 0)
        right = cat([cat([ur, -ui], 1), cat([ui, ur], 1)], 0)
        left = cat([cat([urt, uit], 1), cat([-uit, urt], 1)], 0)
        for c in range(4):
            at = pl.ds(c * quarter + k, WF, stride=half_rows)
            amat[c * PAD : c * PAD + WF, 0:PAD] = y_re[at, :].astype(bf16)
            amat[c * PAD : c * PAD + WF, PAD : 2 * PAD] = y_im[at, :].astype(bf16)
        ht = lax.dot_general(first, amat[...], NT, preferred_element_type=f32).astype(bf16)
        m = cat(
            [
                cat([ht[0:PAD, c * PAD : (c + 1) * PAD], ht[PAD:, c * PAD : (c + 1) * PAD]], 1)
                for c in range(5)
            ],
            0,
        )
        ft = jnp.dot(m, right, preferred_element_type=f32)
        fl = lax.dot_general(left, m, NT, preferred_element_type=f32)
        bre = []
        bim = []
        for c in range(5):
            cs = slice(c * PAD, (c + 1) * PAD)
            bre.append(((fl[0:PAD, cs] + ft[cs, 0:PAD]) * 0.5).astype(bf16))
            bim.append(((fl[PAD:, cs] - ft[cs, PAD:]) * 0.5).astype(bf16))
        hdiag = jnp.where(eye, bre[0].astype(f32), 0.0)
        e_row = jnp.sum(hdiag, axis=0, keepdims=True)
        e_col = jnp.sum(hdiag, axis=1, keepdims=True)
        gap = e_col - e_row
        weight = 1.0 / (gap * gap + broadening * broadening)
        sr = bre[4]
        si = bim[4]
        sl_ = cat([sr, si], 1)
        vr = cat(
            [cat([bre[a], -bim[a]], 0) if j == 0 else cat([bim[a], bre[a]], 0) for a in (1, 2, 3) for j in (0, 1)],
            1,
        )
        prod = jnp.dot(sl_, vr, preferred_element_type=f32)
        vl = cat([cat([bre[a], bim[a]], 1) for a in (1, 2, 3)], 0)
        srhs = cat([cat([sr, si], 1), cat([-si, sr], 1)], 0)
        conj = jnp.dot(vl, srhs, preferred_element_type=f32)
        occ = 1.0 / (1.0 + jnp.exp((e_row - fermi) / smearing))
        wre = [weight * bre[b].astype(f32) for b in (1, 2, 3)]
        wim = [weight * bim[b].astype(f32) for b in (1, 2, 3)]
        for a in range(3):
            c2r = prod[:, 2 * a * PAD : (2 * a + 1) * PAD] + conj[a * PAD : (a + 1) * PAD, 0:PAD]
            c2i = prod[:, (2 * a + 1) * PAD : (2 * a + 2) * PAD] + conj[a * PAD : (a + 1) * PAD, PAD:]
            for b in range(3):
                cv = jnp.sum(c2i * wre[b] - c2r * wim[b], axis=0, keepdims=True)
                p = 3 * a + b
                curv_ref[p, pl.ds(k, 1), :] = cv[:, 0:WF]
                acc[p : p + 1, :] += occ * cv
        return carry

    lax.fori_loop(0, quarter, one_k, 0)

    def red1_copy(step):
        e, dev = peer(step)
        return pltpu.make_async_remote_copy(
            src_ref=acc,
            dst_ref=red1.at[me],
            send_sem=s1.at[step],
            recv_sem=r1.at[step],
            device_id=dev,
            device_id_type=MESH,
        )

    for step in range(1, E):
        red1_copy(step).start()
    red1[me] = acc[...]
    for step in range(1, E):
        red1_copy(step).wait_recv()
    part = red1[0]
    for e in range(1, E):
        part = part + red1[e]
    red2[hi] = part

    def red2_copy(step):
        return pltpu.make_async_remote_copy(
            src_ref=red2.at[hi],
            dst_ref=red2.at[hi],
            send_sem=s2.at[step],
            recv_sem=r2.at[step],
            device_id=line(lax.rem(hi + step, L)),
            device_id_type=MESH,
        )

    for step in range(1, L):
        red2_copy(step).start()
    for step in range(1, L):
        red2_copy(step).wait_recv()
    part = red2[0]
    for u in range(1, L):
        part = part + red2[u]
    total_ref[...] = part[0:9, 0:WF] * (1.0 / math.sqrt(total_points))

    for step in range(1, L):
        red2_copy(step).wait_send()
    for step in range(1, E):
        red1_copy(step).wait_send()
    for n in range(nch):
        for step in range(1, E):
            plane_copy(n, step).wait_send()
            out_copy(n, step).wait_send()
        for d in range(L):

            @pl.when((hi - d >= 0) & (hi + 1 < L))
            def _():
                line_copy(n, hi - d, True).wait_send()

            @pl.when((hi + d < L) & (hi > 0))
            def _():
                line_copy(n, hi + d, False).wait_send()


def on_device(nka, ncol, hamiltonian, eigvecs, spin, k_indices, r_vectors, degeneracy, fermi_level):
    WF = spin.shape[-1]
    L = nka // LO
    E = LO * ncol
    kdev = k_indices.shape[0]
    quarter = kdev // ncol
    rows = hamiltonian.shape[0] * 2
    nr = r_vectors.shape[0]
    width = WF * WF // E
    cw = math.lcm(WF, 128)
    nch = width // cw
    h = hamiltonian.reshape(rows, WF * WF)
    kf = jnp.pad(k_indices.astype(f32), ((0, 0), (0, PAD - 3)))
    rv = r_vectors.astype(f32).T
    inv = 1.0 / degeneracy.astype(f32)[None, :]
    base = jnp.concatenate([rv, jnp.zeros((1, nr), f32), inv, rv * inv], axis=0)
    shift = jnp.zeros((8, 1), f32).at[3].set(GRID // 4)
    table = jnp.stack([base, base + shift], axis=-1).reshape(8, 2 * nr)
    vm = pl.BlockSpec(memory_space=pltpu.VMEM)
    dma = pltpu.SemaphoreType.DMA
    cfg = (WF, L, ncol, rows, nch, cw, kdev, quarter, kdev * nka)
    blk = 8 * quarter
    curv, total = pl.pallas_call(
        functools.partial(kernel, cfg),
        name="spin_hall",
        out_shape=(
            jax.ShapeDtypeStruct((9, quarter, WF), f32),
            jax.ShapeDtypeStruct((9, WF), f32),
        ),
        in_specs=[vm] * 5 + [pl.BlockSpec(memory_space=pltpu.SMEM)],
        out_specs=(vm, vm),
        scratch_shapes=[
            pltpu.VMEM((LO, kdev, PAD), f32),
            pltpu.VMEM((nch, nka * ncol, rows, cw), bf16),
            pltpu.VMEM((E * blk, 2 * nr), bf16),
            pltpu.VMEM((nch, E, blk, cw), bf16),
            pltpu.VMEM((nch, E, blk, cw), bf16),
            pltpu.VMEM((WF * 4 * quarter, PAD), f32),
            pltpu.VMEM((WF * 4 * quarter, PAD), f32),
            pltpu.VMEM((2, PAD, PAD), f32),
            pltpu.VMEM((5 * PAD, 2 * PAD), bf16),
            pltpu.VMEM((16, PAD), f32),
            pltpu.VMEM((E, 16, PAD), f32),
            pltpu.VMEM((L, 16, PAD), f32),
            dma((nch,)),
            dma((3,)),
            dma((nch, E)),
            dma((nch, E)),
            dma((nch, L, 2)),
            dma((nch, L)),
            dma((nch, E)),
            dma((nch, E)),
            dma((E,)),
            dma((E,)),
            dma((L,)),
            dma((L,)),
        ],
        compiler_params=pltpu.CompilerParams(
            collective_id=0, has_side_effects=True, vmem_limit_bytes=60 * 1024 * 1024
        ),
    )(h, eigvecs, spin, kf, table, fermi_level)
    return (jnp.transpose(curv, (0, 2, 1)), total)


def solution(mesh):
    in_specs = (
        P(("ka", "col"), None, None),
        P("ka", None, None, None),
        P(),
        P("ka", None),
        P(),
        P(),
        P(),
    )
    out_specs = (P(None, None, ("ka", "col")), P())
    body = functools.partial(on_device, mesh.shape["ka"], mesh.shape["col"])
    return jax.shard_map(body, mesh=mesh, in_specs=in_specs, out_specs=out_specs, check_vma=False)
```

```python
import functools
import math

import jax
import jax.numpy as jnp
from jax import lax
from jax.experimental import pallas as pl
from jax.experimental.pallas import tpu as pltpu
from jax.sharding import PartitionSpec as P

GRID = 64
broadening = 0.5
smearing = 0.1
LO = 2
PAD = 128
MESH = pl.DeviceIdType.MESH
f32 = jnp.float32
bf16 = jnp.bfloat16


def half_wave(t):
    v = jnp.abs(t - GRID / 2) - GRID / 4
    y = v * (2.0 * math.pi / GRID)
    z = y * y
    p = jnp.full_like(z, 1.0 / 6227020800.0)
    for den in (-39916800.0, 362880.0, -5040.0, 120.0, -6.0):
        p = p * z + 1.0 / den
    return y * (p * z) + y


def kernel(
    cfg,
    h_ref,
    ev_ref,
    spin_ref,
    kf_ref,
    table_ref,
    fermi_ref,
    curv_ref,
    total_ref,
    kall,
    gath,
    phase,
    outs,
    xin,
    y_re,
    y_im,
    upad,
    amat,
    acc,
    red1,
    red2,
    loc_sem,
    k_sem,
    sa,
    ra,
    sl,
    rl,
    so,
    ro,
    s1,
    r1,
    s2,
    r2,
):
    WF, L, ncol, rows, nch, cw, kdev, quarter, total_points = cfg
    E = LO * ncol
    ka = lax.axis_index("ka")
    col = lax.axis_index("col")
    hi = ka // LO
    lo = ka % LO
    me = lo * ncol + col

    def peer(step):
        e = lax.rem(me + step, E)
        return e, (hi * LO + e // ncol, lax.rem(e, ncol))

    def line(h):
        return (h * LO + lo, col)

    pos = lax.rem(hi, 2)
    other = hi + 1 - 2 * pos
    outer = lax.rem(hi // 2 + pos, 2) == 0

    def far(step):
        e, _ = peer(step)
        return e, (other * LO + e // ncol, lax.rem(e, ncol))

    def mine(n):
        return outer if n == 0 else jnp.logical_not(outer)

    def top(n):
        return L - 1 if n == 0 else L - 2

    def bot(n):
        return 0 if n == 0 else 1

    order = (1, 0) + tuple(range(2, nch))

    barrier = pltpu.get_barrier_semaphore()
    for step in range(1, E):
        pl.semaphore_signal(barrier, inc=1, device_id=peer(step)[1], device_id_type=MESH)
    for step in range(1, L):
        pl.semaphore_signal(
            barrier, inc=1, device_id=line(lax.rem(hi + step, L)), device_id_type=MESH
        )
    for step in range(1, E):
        pl.semaphore_signal(barrier, inc=1, device_id=far(step)[1], device_id_type=MESH)
    pl.semaphore_wait(barrier, E - 1 + L - 1 + E - 1)

    src_me = hi * E + me

    def plane_copy(n, step):
        e, dev = peer(step)
        return pltpu.make_async_remote_copy(
            src_ref=h_ref.at[:, pl.ds(pl.multiple_of(e * (nch * cw) + n * cw, 128), cw)],
            dst_ref=gath.at[n, src_me],
            send_sem=sa.at[n, step],
            recv_sem=ra.at[n, step],
            device_id=dev,
            device_id_type=MESH,
        )

    def plane_local(n):
        return pltpu.make_async_copy(
            h_ref.at[:, pl.ds(pl.multiple_of(me * (nch * cw) + n * cw, 128), cw)],
            gath.at[n, src_me],
            loc_sem.at[n],
        )

    def line_copy(n, unit, up):
        tgt = hi + 1 if up else hi - 1
        return pltpu.make_async_remote_copy(
            src_ref=gath.at[n, pl.ds(unit * E, E)],
            dst_ref=gath.at[n, pl.ds(unit * E, E)],
            send_sem=sl.at[n, unit, 0 if up else 1],
            recv_sem=rl.at[n, unit],
            device_id=line(tgt),
            device_id_type=MESH,
        )

    def k_copy(j):
        h = hi if j == 1 else other
        low = lo if j == 2 else 1 - lo
        return pltpu.make_async_remote_copy(
            src_ref=kf_ref,
            dst_ref=kall.at[pos * LO + lo],
            send_sem=k_sem.at[0, j],
            recv_sem=k_sem.at[1, j],
            device_id=(h * LO + low, col),
            device_id_type=MESH,
        )

    k_local = pltpu.make_async_copy(kf_ref, kall.at[pos * LO + lo], k_sem.at[0, 0])
    k_local.start()
    for j in (1, 2, 3):
        k_copy(j).start()
    for n in order:
        plane_local(n).start()
        for step in range(1, E):
            plane_copy(n, step).start()

    def own_units(n):
        plane_local(n).wait()
        for step in range(1, E):
            plane_copy(n, step).wait_recv()

        @pl.when(hi + 1 <= top(n))
        def _():
            line_copy(n, hi, True).start()

        @pl.when(hi - 1 >= bot(n))
        def _():
            line_copy(n, hi, False).start()

    def forward(n, d):
        @pl.when((hi - d >= 0) & (hi <= top(n)))
        def _():
            line_copy(n, hi - d, True).wait_recv()

            @pl.when(hi + 1 <= top(n))
            def _():
                line_copy(n, hi - d, True).start()

        @pl.when((hi + d < L) & (hi >= bot(n)))
        def _():
            line_copy(n, hi + d, False).wait_recv()

            @pl.when(hi - 1 >= bot(n))
            def _():
                line_copy(n, hi + d, False).start()

    for n in order:
        own_units(n)

    k_local.wait()
    for j in (1, 2, 3):
        k_copy(j).wait()
    y_re[...] = jnp.zeros_like(y_re)
    y_im[...] = jnp.zeros_like(y_im)
    upad[...] = jnp.zeros_like(upad)
    amat[...] = jnp.zeros_like(amat)
    acc[...] = jnp.zeros_like(acc)
    sre = spin_ref[0].astype(f32)
    sim = spin_ref[1].astype(f32)
    upad[0, 0:WF, 0:WF] = sre
    upad[1, 0:WF, 0:WF] = sim
    sre = upad[0]
    sim = upad[1]
    amat[4 * PAD : 5 * PAD, 0:PAD] = ((sre + sre.T) * 0.5).astype(bf16)
    amat[4 * PAD : 5 * PAD, PAD : 2 * PAD] = ((sim - sim.T) * 0.5).astype(bf16)

    lanes = table_ref.shape[1]
    lw = 512 if lanes % 512 == 0 else 128
    per_lo = kdev // quarter

    def phase_body(idx, carry):
        dest = idx // (lanes // lw)
        off = pl.multiple_of(lax.rem(idx, lanes // lw) * lw, 128)
        kk = kall[dest // per_lo, pl.ds(pl.multiple_of(lax.rem(dest, per_lo) * quarter, 8), quarter), :]
        tab = table_ref[:, pl.ds(off, lw)]
        dot = (
            kk[:, 0:1] * tab[0:1, :]
            + kk[:, 1:2] * tab[1:2, :]
            + kk[:, 2:3] * tab[2:3, :]
            + tab[3:4, :]
        )
        t = dot - GRID * jnp.floor(dot * (1.0 / GRID))
        tq = t + (3 * GRID // 4)
        tq = jnp.where(tq >= GRID, tq - GRID, tq)
        cosine = half_wave(t)
        sine = half_wave(tq)
        base = pl.multiple_of(dest * (8 * quarter), 16)
        for c in range(4):
            if c == 0:
                top = cosine * tab[4:5, :]
                low = sine * tab[4:5, :]
            else:
                top = -sine * tab[4 + c : 5 + c, :]
                low = cosine * tab[4 + c : 5 + c, :]
            phase[pl.ds(base + c * quarter, quarter), pl.ds(off, lw)] = top.astype(bf16)
            phase[pl.ds(base + (4 + c) * quarter, quarter), pl.ds(off, lw)] = low.astype(bf16)
        return carry

    lax.fori_loop(0, 2 * E * (lanes // lw), phase_body, 0)

    def out_copy(n, step, away):
        e, dev = far(step) if away else peer(step)
        return pltpu.make_async_remote_copy(
            src_ref=outs.at[n, 1 if away else 0, e],
            dst_ref=xin.at[n, me],
            send_sem=so.at[n, 1 if away else 0, step],
            recv_sem=ro.at[n, step],
            device_id=dev,
            device_id_type=MESH,
        )

    blk = 8 * quarter

    def multiply(n):
        def block(plane, e):
            at = pl.ds(pl.multiple_of((plane * E + e) * blk, 16), blk)
            return jnp.dot(
                phase[at, :], gath[n].reshape(lanes, cw), preferred_element_type=f32
            ).astype(bf16)

        def mm_far(step, carry):
            e = lax.rem(me + step, E)
            outs[n, 1, e] = block(1 - pos, e)
            out_copy(n, step, True).start()
            return carry

        def mm_near(step, carry):
            e = lax.rem(me + step, E)
            outs[n, 0, e] = block(pos, e)
            out_copy(n, step, False).start()
            return carry

        lax.fori_loop(0, E, mm_far, 0)
        lax.fori_loop(1, E, mm_near, 0)
        xin[n, me] = block(pos, me)

    for n in order:
        for d in range(1, L):
            forward(n, d)

        @pl.when(mine(n))
        def _(n=n):
            multiply(n)

    half_rows = 4 * quarter
    per = cw // WF
    for n in order:
        for step in range(1, E):
            out_copy(n, step, False).wait_recv()

        @pl.when(jnp.logical_not(mine(n)))
        def _(n=n):
            out_copy(n, 0, True).wait_recv()

        def unflat(e, carry, n=n):
            x = xin[n, e].astype(f32)
            for q in range(per):
                i = e * (nch * per) + n * per + q
                at = pl.ds(pl.multiple_of(i * half_rows, 8), half_rows)
                y_re[at, 0:WF] = x[0:half_rows, q * WF : (q + 1) * WF]
                y_im[at, 0:WF] = x[half_rows:, q * WF : (q + 1) * WF]
            return carry

        lax.fori_loop(0, E, unflat, 0)

    row = lax.broadcasted_iota(jnp.int32, (PAD, PAD), 0)
    lane = lax.broadcasted_iota(jnp.int32, (PAD, PAD), 1)
    eye = row == lane
    fermi = fermi_ref[0]
    NT = (((1,), (1,)), ((), ()))

    def one_k(k, carry):
        upad[0, 0:WF, 0:WF] = ev_ref[col * quarter + k, 0].astype(f32)
        upad[1, 0:WF, 0:WF] = ev_ref[col * quarter + k, 1].astype(f32)
        ur = upad[0]
        ui = upad[1]
        urt = ur.T.astype(bf16)
        uit = ui.T.astype(bf16)
        ur = ur.astype(bf16)
        ui = ui.astype(bf16)
        cat = jnp.concatenate
        first = cat([cat([urt, -uit], 1), cat([uit, urt], 1)], 0)
        right = cat([cat([ur, -ui], 1), cat([ui, ur], 1)], 0)
        left = cat([cat([urt, uit], 1), cat([-uit, urt], 1)], 0)
        for c in range(4):
            at = pl.ds(c * quarter + k, WF, stride=half_rows)
            amat[c * PAD : c * PAD + WF, 0:PAD] = y_re[at, :].astype(bf16)
            amat[c * PAD : c * PAD + WF, PAD : 2 * PAD] = y_im[at, :].astype(bf16)
        ht = lax.dot_general(first, amat[...], NT, preferred_element_type=f32).astype(bf16)
        m = cat(
            [
                cat([ht[0:PAD, c * PAD : (c + 1) * PAD], ht[PAD:, c * PAD : (c + 1) * PAD]], 1)
                for c in range(5)
            ],
            0,
        )
        ft = jnp.dot(m, right, preferred_element_type=f32)
        fl = lax.dot_general(left, m, NT, preferred_element_type=f32)
        bre = []
        bim = []
        for c in range(5):
            cs = slice(c * PAD, (c + 1) * PAD)
            bre.append(((fl[0:PAD, cs] + ft[cs, 0:PAD]) * 0.5).astype(bf16))
            bim.append(((fl[PAD:, cs] - ft[cs, PAD:]) * 0.5).astype(bf16))
        hdiag = jnp.where(eye, bre[0].astype(f32), 0.0)
        e_row = jnp.sum(hdiag, axis=0, keepdims=True)
        e_col = jnp.sum(hdiag, axis=1, keepdims=True)
        gap = e_col - e_row
        weight = 1.0 / (gap * gap + broadening * broadening)
        sr = bre[4]
        si = bim[4]
        sl_ = cat([sr, si], 1)
        vr = cat(
            [cat([bre[a], -bim[a]], 0) if j == 0 else cat([bim[a], bre[a]], 0) for a in (1, 2, 3) for j in (0, 1)],
            1,
        )
        prod = jnp.dot(sl_, vr, preferred_element_type=f32)
        vl = cat([cat([bre[a], bim[a]], 1) for a in (1, 2, 3)], 0)
        srhs = cat([cat([sr, si], 1), cat([-si, sr], 1)], 0)
        conj = jnp.dot(vl, srhs, preferred_element_type=f32)
        occ = 1.0 / (1.0 + jnp.exp((e_row - fermi) / smearing))
        wre = [weight * bre[b].astype(f32) for b in (1, 2, 3)]
        wim = [weight * bim[b].astype(f32) for b in (1, 2, 3)]
        for a in range(3):
            c2r = prod[:, 2 * a * PAD : (2 * a + 1) * PAD] + conj[a * PAD : (a + 1) * PAD, 0:PAD]
            c2i = prod[:, (2 * a + 1) * PAD : (2 * a + 2) * PAD] + conj[a * PAD : (a + 1) * PAD, PAD:]
            for b in range(3):
                cv = jnp.sum(c2i * wre[b] - c2r * wim[b], axis=0, keepdims=True)
                p = 3 * a + b
                curv_ref[p, pl.ds(k, 1), :] = cv[:, 0:WF]
                acc[p : p + 1, :] += occ * cv
        return carry

    lax.fori_loop(0, quarter, one_k, 0)

    def red1_copy(step):
        e, dev = peer(step)
        return pltpu.make_async_remote_copy(
            src_ref=acc,
            dst_ref=red1.at[me],
            send_sem=s1.at[step],
            recv_sem=r1.at[step],
            device_id=dev,
            device_id_type=MESH,
        )

    for step in range(1, E):
        red1_copy(step).start()
    red1[me] = acc[...]
    for step in range(1, E):
        red1_copy(step).wait_recv()
    part = red1[0]
    for e in range(1, E):
        part = part + red1[e]
    red2[hi] = part

    def red2_copy(step):
        return pltpu.make_async_remote_copy(
            src_ref=red2.at[hi],
            dst_ref=red2.at[hi],
            send_sem=s2.at[step],
            recv_sem=r2.at[step],
            device_id=line(lax.rem(hi + step, L)),
            device_id_type=MESH,
        )

    for step in range(1, L):
        red2_copy(step).start()
    for step in range(1, L):
        red2_copy(step).wait_recv()
    part = red2[0]
    for u in range(1, L):
        part = part + red2[u]
    total_ref[...] = part[0:9, 0:WF] * (1.0 / math.sqrt(total_points))

    for step in range(1, L):
        red2_copy(step).wait_send()
    for step in range(1, E):
        red1_copy(step).wait_send()
    for n in range(nch):
        for step in range(1, E):
            plane_copy(n, step).wait_send()

        @pl.when(mine(n))
        def _(n=n):
            for step in range(E):
                out_copy(n, step, True).wait_send()
            for step in range(1, E):
                out_copy(n, step, False).wait_send()

        for d in range(L):

            @pl.when((hi - d >= 0) & (hi + 1 <= top(n)))
            def _(n=n, d=d):
                line_copy(n, hi - d, True).wait_send()

            @pl.when((hi + d < L) & (hi - 1 >= bot(n)))
            def _(n=n, d=d):
                line_copy(n, hi + d, False).wait_send()


def on_device(nka, ncol, hamiltonian, eigvecs, spin, k_indices, r_vectors, degeneracy, fermi_level):
    WF = spin.shape[-1]
    L = nka // LO
    E = LO * ncol
    kdev = k_indices.shape[0]
    quarter = kdev // ncol
    rows = hamiltonian.shape[0] * 2
    nr = r_vectors.shape[0]
    width = WF * WF // E
    cw = math.lcm(WF, 128)
    nch = width // cw
    h = hamiltonian.reshape(rows, WF * WF)
    kf = jnp.pad(k_indices.astype(f32), ((0, 0), (0, PAD - 3)))
    rv = r_vectors.astype(f32).T
    inv = 1.0 / degeneracy.astype(f32)[None, :]
    base = jnp.concatenate([rv, jnp.zeros((1, nr), f32), inv, rv * inv], axis=0)
    shift = jnp.zeros((8, 1), f32).at[3].set(GRID // 4)
    table = jnp.stack([base, base + shift], axis=-1).reshape(8, 2 * nr)
    vm = pl.BlockSpec(memory_space=pltpu.VMEM)
    dma = pltpu.SemaphoreType.DMA
    cfg = (WF, L, ncol, rows, nch, cw, kdev, quarter, kdev * nka)
    blk = 8 * quarter
    curv, total = pl.pallas_call(
        functools.partial(kernel, cfg),
        name="spin_hall",
        out_shape=(
            jax.ShapeDtypeStruct((9, quarter, WF), f32),
            jax.ShapeDtypeStruct((9, WF), f32),
        ),
        in_specs=[vm] * 5 + [pl.BlockSpec(memory_space=pltpu.SMEM)],
        out_specs=(vm, vm),
        scratch_shapes=[
            pltpu.VMEM((2 * LO, kdev, PAD), f32),
            pltpu.VMEM((nch, nka * ncol, rows, cw), bf16),
            pltpu.VMEM((2 * E * blk, 2 * nr), bf16),
            pltpu.VMEM((nch, 2, E, blk, cw), bf16),
            pltpu.VMEM((nch, E, blk, cw), bf16),
            pltpu.VMEM((WF * 4 * quarter, PAD), f32),
            pltpu.VMEM((WF * 4 * quarter, PAD), f32),
            pltpu.VMEM((2, PAD, PAD), f32),
            pltpu.VMEM((5 * PAD, 2 * PAD), bf16),
            pltpu.VMEM((16, PAD), f32),
            pltpu.VMEM((E, 16, PAD), f32),
            pltpu.VMEM((L, 16, PAD), f32),
            dma((nch,)),
            dma((2, 4)),
            dma((nch, E)),
            dma((nch, E)),
            dma((nch, L, 2)),
            dma((nch, L)),
            dma((nch, 2, E)),
            dma((nch, E)),
            dma((E,)),
            dma((E,)),
            dma((L,)),
            dma((L,)),
        ],
        compiler_params=pltpu.CompilerParams(
            collective_id=0, has_side_effects=True, vmem_limit_bytes=60 * 1024 * 1024
        ),
    )(h, eigvecs, spin, kf, table, fermi_level)
    return (jnp.transpose(curv, (0, 2, 1)), total)


def solution(mesh):
    in_specs = (
        P(("ka", "col"), None, None),
        P("ka", None, None, None),
        P(),
        P("ka", None),
        P(),
        P(),
        P(),
    )
    out_specs = (P(None, None, ("ka", "col")), P())
    body = functools.partial(on_device, mesh.shape["ka"], mesh.shape["col"])
    return jax.shard_map(body, mesh=mesh, in_specs=in_specs, out_specs=out_specs, check_vma=False)
```

```python
import functools
import math

import jax
import jax.numpy as jnp
from jax import lax
from jax.experimental import pallas as pl
from jax.experimental.pallas import tpu as pltpu
from jax.sharding import PartitionSpec as P

GRID = 64
broadening = 0.5
smearing = 0.1
LO = 2
PAD = 128
MESH = pl.DeviceIdType.MESH
f32 = jnp.float32
bf16 = jnp.bfloat16


def half_wave(t):
    v = jnp.abs(t - GRID / 2) - GRID / 4
    y = v * (2.0 * math.pi / GRID)
    z = y * y
    p = jnp.full_like(z, 1.0 / 6227020800.0)
    for den in (-39916800.0, 362880.0, -5040.0, 120.0, -6.0):
        p = p * z + 1.0 / den
    return y * (p * z) + y


def kernel(
    cfg,
    h_ref,
    ev_ref,
    spin_ref,
    kt_ref,
    rt_ref,
    deg_ref,
    fermi_ref,
    curv_ref,
    total_ref,
    table_ref,
    kall,
    gath,
    phase,
    outs,
    xin,
    y_re,
    y_im,
    upad,
    amat,
    acc,
    red1,
    red2,
    loc_sem,
    k_sem,
    sa,
    ra,
    sl,
    rl,
    so,
    ro,
    s1,
    r1,
    s2,
    r2,
):
    WF, L, ncol, rows, nch, cw, kdev, quarter, total_points = cfg
    E = LO * ncol
    ka = lax.axis_index("ka")
    col = lax.axis_index("col")
    hi = ka // LO
    lo = ka % LO
    me = lo * ncol + col

    def peer(step):
        e = lax.rem(me + step, E)
        return e, (hi * LO + e // ncol, lax.rem(e, ncol))

    def line(h):
        return (h * LO + lo, col)

    pos = lax.rem(hi, 2)
    other = hi + 1 - 2 * pos
    outer = lax.rem(hi // 2 + pos, 2) == 0

    def far(step):
        e, _ = peer(step)
        return e, (other * LO + e // ncol, lax.rem(e, ncol))

    def mine(n):
        return outer if n == 0 else jnp.logical_not(outer)

    def top(n):
        return L - 1 if n == 0 else L - 2

    def bot(n):
        return 0 if n == 0 else 1

    order = tuple(range(nch))

    barrier = pltpu.get_barrier_semaphore()
    for step in range(1, E):
        pl.semaphore_signal(barrier, inc=1, device_id=peer(step)[1], device_id_type=MESH)
    for step in range(1, L):
        pl.semaphore_signal(
            barrier, inc=1, device_id=line(lax.rem(hi + step, L)), device_id_type=MESH
        )
    for step in range(1, E):
        pl.semaphore_signal(barrier, inc=1, device_id=far(step)[1], device_id_type=MESH)
    pl.semaphore_wait(barrier, E - 1 + L - 1 + E - 1)

    src_me = hi * E + me

    def plane_copy(n, step):
        e, dev = peer(step)
        return pltpu.make_async_remote_copy(
            src_ref=h_ref.at[:, pl.ds(pl.multiple_of(e * (nch * cw) + n * cw, 128), cw)],
            dst_ref=gath.at[n, src_me],
            send_sem=sa.at[n, step],
            recv_sem=ra.at[n, step],
            device_id=dev,
            device_id_type=MESH,
        )

    def plane_local(n):
        return pltpu.make_async_copy(
            h_ref.at[:, pl.ds(pl.multiple_of(me * (nch * cw) + n * cw, 128), cw)],
            gath.at[n, src_me],
            loc_sem.at[n],
        )

    def line_copy(n, unit, up):
        tgt = hi + 1 if up else hi - 1
        return pltpu.make_async_remote_copy(
            src_ref=gath.at[n, pl.ds(unit * E, E)],
            dst_ref=gath.at[n, pl.ds(unit * E, E)],
            send_sem=sl.at[n, unit, 0 if up else 1],
            recv_sem=rl.at[n, unit],
            device_id=line(tgt),
            device_id_type=MESH,
        )

    def k_copy(j):
        h = hi if j == 1 else other
        low = lo if j == 2 else 1 - lo
        return pltpu.make_async_remote_copy(
            src_ref=kall.at[pos * LO + lo],
            dst_ref=kall.at[pos * LO + lo],
            send_sem=k_sem.at[0, j],
            recv_sem=k_sem.at[1, j],
            device_id=(h * LO + low, col),
            device_id_type=MESH,
        )

    upad[...] = jnp.zeros_like(upad)
    upad[0, 0:3, 0:kdev] = kt_ref[...].astype(f32)
    kall[pos * LO + lo] = upad[0].T[0:kdev, :]
    for j in (1, 2, 3):
        k_copy(j).start()
    for n in order:
        plane_local(n).start()
        for step in range(1, E):
            plane_copy(n, step).start()

    def own_units(n):
        plane_local(n).wait()
        for step in range(1, E):
            plane_copy(n, step).wait_recv()

        @pl.when(hi + 1 <= top(n))
        def _():
            line_copy(n, hi, True).start()

        @pl.when(hi - 1 >= bot(n))
        def _():
            line_copy(n, hi, False).start()

    def forward(n, d):
        @pl.when((hi - d >= 0) & (hi <= top(n)))
        def _():
            line_copy(n, hi - d, True).wait_recv()

            @pl.when(hi + 1 <= top(n))
            def _():
                line_copy(n, hi - d, True).start()

        @pl.when((hi + d < L) & (hi >= bot(n)))
        def _():
            line_copy(n, hi + d, False).wait_recv()

            @pl.when(hi - 1 >= bot(n))
            def _():
                line_copy(n, hi + d, False).start()

    for n in order:
        own_units(n)

    for j in (1, 2, 3):
        k_copy(j).wait()
    y_re[...] = jnp.zeros_like(y_re)
    y_im[...] = jnp.zeros_like(y_im)
    upad[...] = jnp.zeros_like(upad)
    amat[...] = jnp.zeros_like(amat)
    acc[...] = jnp.zeros_like(acc)
    sre = spin_ref[0].astype(f32)
    sim = spin_ref[1].astype(f32)
    upad[0, 0:WF, 0:WF] = sre
    upad[1, 0:WF, 0:WF] = sim
    sre = upad[0]
    sim = upad[1]
    amat[4 * PAD : 5 * PAD, 0:PAD] = ((sre + sre.T) * 0.5).astype(bf16)
    amat[4 * PAD : 5 * PAD, PAD : 2 * PAD] = ((sim - sim.T) * 0.5).astype(bf16)

    lanes = table_ref.shape[1]
    wide = lax.broadcasted_iota(jnp.int32, (PAD, 2 * PAD), 1)
    deep = lax.broadcasted_iota(jnp.int32, (PAD, 2 * PAD), 0)
    twice = jnp.where(wide // 2 == deep, 1.0, 0.0).astype(bf16)
    nr = lanes // 2
    rvec = jnp.concatenate(
        [rt_ref[...].astype(f32), deg_ref[...].astype(f32), jnp.zeros((4, nr), f32)], axis=0
    ).astype(bf16)
    odd = (lax.broadcasted_iota(jnp.int32, (1, 2 * PAD), 1) % 2).astype(f32)
    for j in range(nr // PAD):
        both = jnp.dot(rvec[:, j * PAD : (j + 1) * PAD], twice, preferred_element_type=f32)
        inv = 1.0 / both[3:4, :]
        js = slice(2 * j * PAD, 2 * (j + 1) * PAD)
        table_ref[0:3, js] = both[0:3, :]
        table_ref[3:4, js] = odd * (GRID // 4)
        table_ref[4:5, js] = inv
        table_ref[5:8, js] = both[0:3, :] * inv
    lw = 512 if lanes % 512 == 0 else 128
    per_lo = kdev // quarter

    def phase_body(idx, carry):
        dest = idx // (lanes // lw)
        off = pl.multiple_of(lax.rem(idx, lanes // lw) * lw, 128)
        kk = kall[dest // per_lo, pl.ds(pl.multiple_of(lax.rem(dest, per_lo) * quarter, 8), quarter), :]
        tab = table_ref[:, pl.ds(off, lw)]
        dot = (
            kk[:, 0:1] * tab[0:1, :]
            + kk[:, 1:2] * tab[1:2, :]
            + kk[:, 2:3] * tab[2:3, :]
            + tab[3:4, :]
        )
        t = dot - GRID * jnp.floor(dot * (1.0 / GRID))
        tq = t + (3 * GRID // 4)
        tq = jnp.where(tq >= GRID, tq - GRID, tq)
        cosine = half_wave(t)
        sine = half_wave(tq)
        base = pl.multiple_of(dest * (8 * quarter), 16)
        for c in range(4):
            if c == 0:
                top = cosine * tab[4:5, :]
                low = sine * tab[4:5, :]
            else:
                top = -sine * tab[4 + c : 5 + c, :]
                low = cosine * tab[4 + c : 5 + c, :]
            phase[pl.ds(base + c * quarter, quarter), pl.ds(off, lw)] = top.astype(bf16)
            phase[pl.ds(base + (4 + c) * quarter, quarter), pl.ds(off, lw)] = low.astype(bf16)
        return carry

    lax.fori_loop(0, 2 * E * (lanes // lw), phase_body, 0)

    def out_copy(n, step, away):
        e, dev = far(step) if away else peer(step)
        return pltpu.make_async_remote_copy(
            src_ref=outs.at[n, 1 if away else 0, e],
            dst_ref=xin.at[n, me],
            send_sem=so.at[n, 1 if away else 0, step],
            recv_sem=ro.at[n, step],
            device_id=dev,
            device_id_type=MESH,
        )

    blk = 8 * quarter

    def multiply(n):
        def block(plane, e):
            at = pl.ds(pl.multiple_of((plane * E + e) * blk, 16), blk)
            return jnp.dot(
                phase[at, :], gath[n].reshape(lanes, cw), preferred_element_type=f32
            ).astype(bf16)

        def mm_far(step, carry):
            e = lax.rem(me + step, E)
            outs[n, 1, e] = block(1 - pos, e)
            out_copy(n, step, True).start()
            return carry

        def mm_near(step, carry):
            e = lax.rem(me + step, E)
            outs[n, 0, e] = block(pos, e)
            out_copy(n, step, False).start()
            return carry

        lax.fori_loop(0, E, mm_far, 0)
        lax.fori_loop(1, E, mm_near, 0)
        xin[n, me] = block(pos, me)

    for n in order:
        for d in range(1, L):
            forward(n, d)

        @pl.when(mine(n))
        def _(n=n):
            multiply(n)

    half_rows = 4 * quarter
    per = cw // WF
    for n in order:
        for step in range(1, E):
            out_copy(n, step, False).wait_recv()

        @pl.when(jnp.logical_not(mine(n)))
        def _(n=n):
            out_copy(n, 0, True).wait_recv()

        def unflat(e, carry, n=n):
            x = xin[n, e].astype(f32)
            for q in range(per):
                i = e * (nch * per) + n * per + q
                at = pl.ds(pl.multiple_of(i * half_rows, 8), half_rows)
                y_re[at, 0:WF] = x[0:half_rows, q * WF : (q + 1) * WF]
                y_im[at, 0:WF] = x[half_rows:, q * WF : (q + 1) * WF]
            return carry

        lax.fori_loop(0, E, unflat, 0)

    row = lax.broadcasted_iota(jnp.int32, (PAD, PAD), 0)
    lane = lax.broadcasted_iota(jnp.int32, (PAD, PAD), 1)
    eye = row == lane
    fermi = fermi_ref[0]
    NT = (((1,), (1,)), ((), ()))

    def one_k(k, carry):
        upad[0, 0:WF, 0:WF] = ev_ref[col * quarter + k, 0].astype(f32)
        upad[1, 0:WF, 0:WF] = ev_ref[col * quarter + k, 1].astype(f32)
        ur = upad[0]
        ui = upad[1]
        urt = ur.T.astype(bf16)
        uit = ui.T.astype(bf16)
        ur = ur.astype(bf16)
        ui = ui.astype(bf16)
        cat = jnp.concatenate
        first = cat([cat([urt, -uit], 1), cat([uit, urt], 1)], 0)
        right = cat([cat([ur, -ui], 1), cat([ui, ur], 1)], 0)
        left = cat([cat([urt, uit], 1), cat([-uit, urt], 1)], 0)
        for c in range(4):
            at = pl.ds(c * quarter + k, WF, stride=half_rows)
            amat[c * PAD : c * PAD + WF, 0:PAD] = y_re[at, :].astype(bf16)
            amat[c * PAD : c * PAD + WF, PAD : 2 * PAD] = y_im[at, :].astype(bf16)
        ht = lax.dot_general(first, amat[...], NT, preferred_element_type=f32).astype(bf16)
        m = cat(
            [
                cat([ht[0:PAD, c * PAD : (c + 1) * PAD], ht[PAD:, c * PAD : (c + 1) * PAD]], 1)
                for c in range(5)
            ],
            0,
        )
        ft = jnp.dot(m, right, preferred_element_type=f32)
        fl = lax.dot_general(left, m, NT, preferred_element_type=f32)
        bre = []
        bim = []
        for c in range(5):
            cs = slice(c * PAD, (c + 1) * PAD)
            bre.append(((fl[0:PAD, cs] + ft[cs, 0:PAD]) * 0.5).astype(bf16))
            bim.append(((fl[PAD:, cs] - ft[cs, PAD:]) * 0.5).astype(bf16))
        hdiag = jnp.where(eye, bre[0].astype(f32), 0.0)
        e_row = jnp.sum(hdiag, axis=0, keepdims=True)
        e_col = jnp.sum(hdiag, axis=1, keepdims=True)
        gap = e_col - e_row
        weight = 1.0 / (gap * gap + broadening * broadening)
        sr = bre[4]
        si = bim[4]
        sl_ = cat([sr, si], 1)
        vr = cat(
            [cat([bre[a], -bim[a]], 0) if j == 0 else cat([bim[a], bre[a]], 0) for a in (1, 2, 3) for j in (0, 1)],
            1,
        )
        prod = jnp.dot(sl_, vr, preferred_element_type=f32)
        vl = cat([cat([bre[a], bim[a]], 1) for a in (1, 2, 3)], 0)
        srhs = cat([cat([sr, si], 1), cat([-si, sr], 1)], 0)
        conj = jnp.dot(vl, srhs, preferred_element_type=f32)
        occ = 1.0 / (1.0 + jnp.exp((e_row - fermi) / smearing))
        wre = [weight * bre[b].astype(f32) for b in (1, 2, 3)]
        wim = [weight * bim[b].astype(f32) for b in (1, 2, 3)]
        for a in range(3):
            c2r = prod[:, 2 * a * PAD : (2 * a + 1) * PAD] + conj[a * PAD : (a + 1) * PAD, 0:PAD]
            c2i = prod[:, (2 * a + 1) * PAD : (2 * a + 2) * PAD] + conj[a * PAD : (a + 1) * PAD, PAD:]
            for b in range(3):
                cv = jnp.sum(c2i * wre[b] - c2r * wim[b], axis=0, keepdims=True)
                p = 3 * a + b
                curv_ref[p, pl.ds(k, 1), :] = cv[:, 0:WF]
                acc[p : p + 1, :] += occ * cv
        return carry

    lax.fori_loop(0, quarter, one_k, 0, unroll=2)

    def red1_copy(step):
        e, dev = peer(step)
        return pltpu.make_async_remote_copy(
            src_ref=acc,
            dst_ref=red1.at[me],
            send_sem=s1.at[step],
            recv_sem=r1.at[step],
            device_id=dev,
            device_id_type=MESH,
        )

    for step in range(1, E):
        red1_copy(step).start()
    red1[me] = acc[...]
    for step in range(1, E):
        red1_copy(step).wait_recv()
    part = red1[0]
    for e in range(1, E):
        part = part + red1[e]
    red2[hi] = part

    def red2_copy(step):
        return pltpu.make_async_remote_copy(
            src_ref=red2.at[hi],
            dst_ref=red2.at[hi],
            send_sem=s2.at[step],
            recv_sem=r2.at[step],
            device_id=line(lax.rem(hi + step, L)),
            device_id_type=MESH,
        )

    for step in range(1, L):
        red2_copy(step).start()
    for step in range(1, L):
        red2_copy(step).wait_recv()
    part = red2[0]
    for u in range(1, L):
        part = part + red2[u]
    total_ref[...] = part[0:9, 0:WF] * (1.0 / math.sqrt(total_points))

    for step in range(1, L):
        red2_copy(step).wait_send()
    for step in range(1, E):
        red1_copy(step).wait_send()
    for n in range(nch):
        for step in range(1, E):
            plane_copy(n, step).wait_send()

        @pl.when(mine(n))
        def _(n=n):
            for step in range(E):
                out_copy(n, step, True).wait_send()
            for step in range(1, E):
                out_copy(n, step, False).wait_send()

        for d in range(L):

            @pl.when((hi - d >= 0) & (hi + 1 <= top(n)))
            def _(n=n, d=d):
                line_copy(n, hi - d, True).wait_send()

            @pl.when((hi + d < L) & (hi - 1 >= bot(n)))
            def _(n=n, d=d):
                line_copy(n, hi + d, False).wait_send()


def on_device(nka, ncol, hamiltonian, eigvecs, spin, k_indices, r_vectors, degeneracy, fermi_level):
    WF = spin.shape[-1]
    L = nka // LO
    E = LO * ncol
    kdev = k_indices.shape[0]
    quarter = kdev // ncol
    rows = hamiltonian.shape[0] * 2
    nr = r_vectors.shape[0]
    width = WF * WF // E
    cw = math.lcm(WF, 128)
    nch = width // cw
    h = hamiltonian.reshape(rows, WF * WF)
    vm = pl.BlockSpec(memory_space=pltpu.VMEM)
    dma = pltpu.SemaphoreType.DMA
    cfg = (WF, L, ncol, rows, nch, cw, kdev, quarter, kdev * nka)
    blk = 8 * quarter
    curv, total = pl.pallas_call(
        functools.partial(kernel, cfg),
        name="spin_hall",
        out_shape=(
            jax.ShapeDtypeStruct((9, quarter, WF), f32),
            jax.ShapeDtypeStruct((9, WF), f32),
        ),
        in_specs=[vm] * 6 + [pl.BlockSpec(memory_space=pltpu.SMEM)],
        out_specs=(vm, vm),
        scratch_shapes=[
            pltpu.VMEM((8, 2 * nr), f32),
            pltpu.VMEM((2 * LO, kdev, PAD), f32),
            pltpu.VMEM((nch, nka * ncol, rows, cw), bf16),
            pltpu.VMEM((2 * E * blk, 2 * nr), bf16),
            pltpu.VMEM((nch, 2, E, blk, cw), bf16),
            pltpu.VMEM((nch, E, blk, cw), bf16),
            pltpu.VMEM((WF * 4 * quarter, PAD), f32),
            pltpu.VMEM((WF * 4 * quarter, PAD), f32),
            pltpu.VMEM((2, PAD, PAD), f32),
            pltpu.VMEM((5 * PAD, 2 * PAD), bf16),
            pltpu.VMEM((16, PAD), f32),
            pltpu.VMEM((E, 16, PAD), f32),
            pltpu.VMEM((L, 16, PAD), f32),
            dma((nch,)),
            dma((2, 4)),
            dma((nch, E)),
            dma((nch, E)),
            dma((nch, L, 2)),
            dma((nch, L)),
            dma((nch, 2, E)),
            dma((nch, E)),
            dma((E,)),
            dma((E,)),
            dma((L,)),
            dma((L,)),
        ],
        compiler_params=pltpu.CompilerParams(
            collective_id=0, has_side_effects=True, vmem_limit_bytes=60 * 1024 * 1024
        ),
    )(h, eigvecs, spin, k_indices.T, r_vectors.T, degeneracy.reshape(1, nr), fermi_level)
    return (jnp.transpose(curv, (0, 2, 1)), total)


def solution(mesh):
    in_specs = (
        P(("ka", "col"), None, None),
        P("ka", None, None, None),
        P(),
        P("ka", None),
        P(),
        P(),
        P(),
    )
    out_specs = (P(None, None, ("ka", "col")), P())
    body = functools.partial(on_device, mesh.shape["ka"], mesh.shape["col"])
    return jax.shard_map(body, mesh=mesh, in_specs=in_specs, out_specs=out_specs, check_vma=False)
```

```python
import functools
import math

import jax
import jax.numpy as jnp
from jax import lax
from jax.experimental import pallas as pl
from jax.experimental.pallas import tpu as pltpu
from jax.sharding import PartitionSpec as P

GRID = 64
broadening = 0.5
smearing = 0.1
LO = 2
PAD = 128
MESH = pl.DeviceIdType.MESH
f32 = jnp.float32
bf16 = jnp.bfloat16


def half_wave(t):
    v = jnp.abs(t - GRID / 2) - GRID / 4
    y = v * (2.0 * math.pi / GRID)
    z = y * y
    p = jnp.full_like(z, 1.0 / 6227020800.0)
    for den in (-39916800.0, 362880.0, -5040.0, 120.0, -6.0):
        p = p * z + 1.0 / den
    return y * (p * z) + y


def kernel(
    cfg,
    h_ref,
    ev_ref,
    spin_ref,
    kt_ref,
    rt_ref,
    deg_ref,
    fermi_ref,
    curv_ref,
    total_ref,
    table_ref,
    kall,
    gath,
    phase,
    outs,
    xin,
    y_re,
    y_im,
    upad,
    amat,
    acc,
    red1,
    red2,
    loc_sem,
    k_sem,
    sa,
    ra,
    sl,
    rl,
    so,
    ro,
    s1,
    r1,
    s2,
    r2,
):
    WF, L, ncol, rows, nch, cw, kdev, quarter, total_points = cfg
    E = LO * ncol
    ka = lax.axis_index("ka")
    col = lax.axis_index("col")
    hi = ka // LO
    lo = ka % LO
    me = lo * ncol + col

    def peer(step):
        e = lax.rem(me + step, E)
        return e, (hi * LO + e // ncol, lax.rem(e, ncol))

    def line(h):
        return (h * LO + lo, col)

    pos = lax.rem(hi, 2)
    other = hi + 1 - 2 * pos
    outer = lax.rem(hi // 2 + pos, 2) == 0

    def far(step):
        e, _ = peer(step)
        return e, (other * LO + e // ncol, lax.rem(e, ncol))

    def mine(n):
        return outer if n == 0 else jnp.logical_not(outer)

    def top(n):
        return L - 1 if n == 0 else L - 2

    def bot(n):
        return 0 if n == 0 else 1

    order = tuple(range(nch))

    barrier = pltpu.get_barrier_semaphore()
    for step in range(1, E):
        pl.semaphore_signal(barrier, inc=1, device_id=peer(step)[1], device_id_type=MESH)
    for step in range(1, L):
        pl.semaphore_signal(
            barrier, inc=1, device_id=line(lax.rem(hi + step, L)), device_id_type=MESH
        )
    for step in range(1, E):
        pl.semaphore_signal(barrier, inc=1, device_id=far(step)[1], device_id_type=MESH)
    pl.semaphore_wait(barrier, E - 1 + L - 1 + E - 1)

    src_me = hi * E + me

    def plane_copy(n, step):
        e, dev = peer(step)
        return pltpu.make_async_remote_copy(
            src_ref=h_ref.at[:, pl.ds(pl.multiple_of(e * (nch * cw) + n * cw, 128), cw)],
            dst_ref=gath.at[n, src_me],
            send_sem=sa.at[n, step],
            recv_sem=ra.at[n, step],
            device_id=dev,
            device_id_type=MESH,
        )

    def plane_local(n):
        return pltpu.make_async_copy(
            h_ref.at[:, pl.ds(pl.multiple_of(me * (nch * cw) + n * cw, 128), cw)],
            gath.at[n, src_me],
            loc_sem.at[n],
        )

    def line_copy(n, unit, up):
        tgt = hi + 1 if up else hi - 1
        return pltpu.make_async_remote_copy(
            src_ref=gath.at[n, pl.ds(unit * E, E)],
            dst_ref=gath.at[n, pl.ds(unit * E, E)],
            send_sem=sl.at[n, unit, 0 if up else 1],
            recv_sem=rl.at[n, unit],
            device_id=line(tgt),
            device_id_type=MESH,
        )

    def k_copy(j):
        h = hi if j == 1 else other
        low = lo if j == 2 else 1 - lo
        return pltpu.make_async_remote_copy(
            src_ref=kall.at[pos * LO + lo],
            dst_ref=kall.at[pos * LO + lo],
            send_sem=k_sem.at[0, j],
            recv_sem=k_sem.at[1, j],
            device_id=(h * LO + low, col),
            device_id_type=MESH,
        )

    upad[...] = jnp.zeros_like(upad)
    upad[0, 0:3, 0:kdev] = kt_ref[...].astype(f32)
    kall[pos * LO + lo] = upad[0].T[0:kdev, :]
    for j in (1, 2, 3):
        k_copy(j).start()
    for n in order:
        plane_local(n).start()
        for step in range(1, E):
            plane_copy(n, step).start()

    def own_units(n):
        plane_local(n).wait()
        for step in range(1, E):
            plane_copy(n, step).wait_recv()

        @pl.when(hi + 1 <= top(n))
        def _():
            line_copy(n, hi, True).start()

        @pl.when(hi - 1 >= bot(n))
        def _():
            line_copy(n, hi, False).start()

    def forward(n, d):
        @pl.when((hi - d >= 0) & (hi <= top(n)))
        def _():
            line_copy(n, hi - d, True).wait_recv()

            @pl.when(hi + 1 <= top(n))
            def _():
                line_copy(n, hi - d, True).start()

        @pl.when((hi + d < L) & (hi >= bot(n)))
        def _():
            line_copy(n, hi + d, False).wait_recv()

            @pl.when(hi - 1 >= bot(n))
            def _():
                line_copy(n, hi + d, False).start()

    for n in order:
        own_units(n)

    forward(0, 1)

    for j in (1, 2, 3):
        k_copy(j).wait()
    y_re[...] = jnp.zeros_like(y_re)
    y_im[...] = jnp.zeros_like(y_im)
    upad[...] = jnp.zeros_like(upad)
    amat[...] = jnp.zeros_like(amat)
    acc[...] = jnp.zeros_like(acc)
    sre = spin_ref[0].astype(f32)
    sim = spin_ref[1].astype(f32)
    upad[0, 0:WF, 0:WF] = sre
    upad[1, 0:WF, 0:WF] = sim
    sre = upad[0]
    sim = upad[1]
    amat[4 * PAD : 5 * PAD, 0:PAD] = ((sre + sre.T) * 0.5).astype(bf16)
    amat[4 * PAD : 5 * PAD, PAD : 2 * PAD] = ((sim - sim.T) * 0.5).astype(bf16)

    lanes = table_ref.shape[1]
    wide = lax.broadcasted_iota(jnp.int32, (PAD, 2 * PAD), 1)
    deep = lax.broadcasted_iota(jnp.int32, (PAD, 2 * PAD), 0)
    twice = jnp.where(wide // 2 == deep, 1.0, 0.0).astype(bf16)
    nr = lanes // 2
    rvec = jnp.concatenate(
        [rt_ref[...].astype(f32), deg_ref[...].astype(f32), jnp.zeros((4, nr), f32)], axis=0
    ).astype(bf16)
    odd = (lax.broadcasted_iota(jnp.int32, (1, 2 * PAD), 1) % 2).astype(f32)
    for j in range(nr // PAD):
        both = jnp.dot(rvec[:, j * PAD : (j + 1) * PAD], twice, preferred_element_type=f32)
        inv = 1.0 / both[3:4, :]
        js = slice(2 * j * PAD, 2 * (j + 1) * PAD)
        table_ref[0:3, js] = both[0:3, :]
        table_ref[3:4, js] = odd * (GRID // 4)
        table_ref[4:5, js] = inv
        table_ref[5:8, js] = both[0:3, :] * inv
    lw = 512 if lanes % 512 == 0 else 128
    per_lo = kdev // quarter

    def phase_body(idx, carry):
        dest = idx // (lanes // lw)
        off = pl.multiple_of(lax.rem(idx, lanes // lw) * lw, 128)
        kk = kall[dest // per_lo, pl.ds(pl.multiple_of(lax.rem(dest, per_lo) * quarter, 8), quarter), :]
        tab = table_ref[:, pl.ds(off, lw)]
        dot = (
            kk[:, 0:1] * tab[0:1, :]
            + kk[:, 1:2] * tab[1:2, :]
            + kk[:, 2:3] * tab[2:3, :]
            + tab[3:4, :]
        )
        t = dot - GRID * jnp.floor(dot * (1.0 / GRID))
        tq = t + (3 * GRID // 4)
        tq = jnp.where(tq >= GRID, tq - GRID, tq)
        cosine = half_wave(t)
        sine = half_wave(tq)
        base = pl.multiple_of(dest * (8 * quarter), 16)
        for c in range(4):
            if c == 0:
                top = cosine * tab[4:5, :]
                low = sine * tab[4:5, :]
            else:
                top = -sine * tab[4 + c : 5 + c, :]
                low = cosine * tab[4 + c : 5 + c, :]
            phase[pl.ds(base + c * quarter, quarter), pl.ds(off, lw)] = top.astype(bf16)
            phase[pl.ds(base + (4 + c) * quarter, quarter), pl.ds(off, lw)] = low.astype(bf16)
        return carry

    lax.fori_loop(0, 2 * E * (lanes // lw), phase_body, 0)

    def out_copy(n, step, away):
        e, dev = far(step) if away else peer(step)
        return pltpu.make_async_remote_copy(
            src_ref=outs.at[n, 1 if away else 0, e],
            dst_ref=xin.at[n, me],
            send_sem=so.at[n, 1 if away else 0, step],
            recv_sem=ro.at[n, step],
            device_id=dev,
            device_id_type=MESH,
        )

    blk = 8 * quarter

    def multiply(n):
        def block(plane, e):
            at = pl.ds(pl.multiple_of((plane * E + e) * blk, 16), blk)
            return jnp.dot(
                phase[at, :], gath[n].reshape(lanes, cw), preferred_element_type=f32
            ).astype(bf16)

        def mm_far(step, carry):
            e = lax.rem(me + step, E)
            outs[n, 1, e] = block(1 - pos, e)
            out_copy(n, step, True).start()
            return carry

        def mm_near(step, carry):
            e = lax.rem(me + step, E)
            outs[n, 0, e] = block(pos, e)
            out_copy(n, step, False).start()
            return carry

        lax.fori_loop(0, E, mm_far, 0)
        lax.fori_loop(1, E, mm_near, 0)
        xin[n, me] = block(pos, me)

    for n in order:
        for d in range(2, L):
            forward(n, d)
        if n + 1 < nch:
            forward(n + 1, 1)

        @pl.when(mine(n))
        def _(n=n):
            multiply(n)

    half_rows = 4 * quarter
    per = cw // WF
    for n in order:
        for step in range(1, E):
            out_copy(n, step, False).wait_recv()

        @pl.when(jnp.logical_not(mine(n)))
        def _(n=n):
            out_copy(n, 0, True).wait_recv()

        def unflat(e, carry, n=n):
            x = xin[n, e].astype(f32)
            for q in range(per):
                i = e * (nch * per) + n * per + q
                at = pl.ds(pl.multiple_of(i * half_rows, 8), half_rows)
                y_re[at, 0:WF] = x[0:half_rows, q * WF : (q + 1) * WF]
                y_im[at, 0:WF] = x[half_rows:, q * WF : (q + 1) * WF]
            return carry

        lax.fori_loop(0, E, unflat, 0)

    row = lax.broadcasted_iota(jnp.int32, (PAD, PAD), 0)
    lane = lax.broadcasted_iota(jnp.int32, (PAD, PAD), 1)
    eye = row == lane
    fermi = fermi_ref[0]
    NT = (((1,), (1,)), ((), ()))

    def one_k(k, carry):
        upad[0, 0:WF, 0:WF] = ev_ref[col * quarter + k, 0].astype(f32)
        upad[1, 0:WF, 0:WF] = ev_ref[col * quarter + k, 1].astype(f32)
        ur = upad[0]
        ui = upad[1]
        urt = ur.T.astype(bf16)
        uit = ui.T.astype(bf16)
        ur = ur.astype(bf16)
        ui = ui.astype(bf16)
        cat = jnp.concatenate
        first = cat([cat([urt, -uit], 1), cat([uit, urt], 1)], 0)
        right = cat([cat([ur, -ui], 1), cat([ui, ur], 1)], 0)
        left = cat([cat([urt, uit], 1), cat([-uit, urt], 1)], 0)
        for c in range(4):
            at = pl.ds(c * quarter + k, WF, stride=half_rows)
            amat[c * PAD : c * PAD + WF, 0:PAD] = y_re[at, :].astype(bf16)
            amat[c * PAD : c * PAD + WF, PAD : 2 * PAD] = y_im[at, :].astype(bf16)
        ht = lax.dot_general(first, amat[...], NT, preferred_element_type=f32).astype(bf16)
        m = cat(
            [
                cat([ht[0:PAD, c * PAD : (c + 1) * PAD], ht[PAD:, c * PAD : (c + 1) * PAD]], 1)
                for c in range(5)
            ],
            0,
        )
        ft = jnp.dot(m, right, preferred_element_type=f32)
        fl = lax.dot_general(left, m, NT, preferred_element_type=f32)
        bre = []
        bim = []
        for c in range(5):
            cs = slice(c * PAD, (c + 1) * PAD)
            bre.append(((fl[0:PAD, cs] + ft[cs, 0:PAD]) * 0.5).astype(bf16))
            bim.append(((fl[PAD:, cs] - ft[cs, PAD:]) * 0.5).astype(bf16))
        hdiag = jnp.where(eye, bre[0].astype(f32), 0.0)
        e_row = jnp.sum(hdiag, axis=0, keepdims=True)
        e_col = jnp.sum(hdiag, axis=1, keepdims=True)
        gap = e_col - e_row
        weight = 1.0 / (gap * gap + broadening * broadening)
        sr = bre[4]
        si = bim[4]
        sl_ = cat([sr, si], 1)
        vr = cat(
            [cat([bre[a], -bim[a]], 0) if j == 0 else cat([bim[a], bre[a]], 0) for a in (1, 2, 3) for j in (0, 1)],
            1,
        )
        prod = jnp.dot(sl_, vr, preferred_element_type=f32)
        vl = cat([cat([bre[a], bim[a]], 1) for a in (1, 2, 3)], 0)
        srhs = cat([cat([sr, si], 1), cat([-si, sr], 1)], 0)
        conj = jnp.dot(vl, srhs, preferred_element_type=f32)
        occ = 1.0 / (1.0 + jnp.exp((e_row - fermi) / smearing))
        wre = [weight * bre[b].astype(f32) for b in (1, 2, 3)]
        wim = [weight * bim[b].astype(f32) for b in (1, 2, 3)]
        for a in range(3):
            c2r = prod[:, 2 * a * PAD : (2 * a + 1) * PAD] + conj[a * PAD : (a + 1) * PAD, 0:PAD]
            c2i = prod[:, (2 * a + 1) * PAD : (2 * a + 2) * PAD] + conj[a * PAD : (a + 1) * PAD, PAD:]
            for b in range(3):
                cv = jnp.sum(c2i * wre[b] - c2r * wim[b], axis=0, keepdims=True)
                p = 3 * a + b
                curv_ref[p, pl.ds(k, 1), :] = cv[:, 0:WF]
                acc[p : p + 1, :] += occ * cv
        return carry

    lax.fori_loop(0, quarter, one_k, 0, unroll=4)

    def red1_copy(step):
        e, dev = peer(step)
        return pltpu.make_async_remote_copy(
            src_ref=acc,
            dst_ref=red1.at[me],
            send_sem=s1.at[step],
            recv_sem=r1.at[step],
            device_id=dev,
            device_id_type=MESH,
        )

    for step in range(1, E):
        red1_copy(step).start()
    red1[me] = acc[...]
    for step in range(1, E):
        red1_copy(step).wait_recv()
    part = red1[0]
    for e in range(1, E):
        part = part + red1[e]
    red2[hi] = part

    def red2_copy(step):
        return pltpu.make_async_remote_copy(
            src_ref=red2.at[hi],
            dst_ref=red2.at[hi],
            send_sem=s2.at[step],
            recv_sem=r2.at[step],
            device_id=line(lax.rem(hi + step, L)),
            device_id_type=MESH,
        )

    for step in range(1, L):
        red2_copy(step).start()
    for step in range(1, L):
        red2_copy(step).wait_recv()
    part = red2[0]
    for u in range(1, L):
        part = part + red2[u]
    total_ref[...] = part[0:9, 0:WF] * (1.0 / math.sqrt(total_points))

    for step in range(1, L):
        red2_copy(step).wait_send()
    for step in range(1, E):
        red1_copy(step).wait_send()
    for n in range(nch):
        for step in range(1, E):
            plane_copy(n, step).wait_send()

        @pl.when(mine(n))
        def _(n=n):
            for step in range(E):
                out_copy(n, step, True).wait_send()
            for step in range(1, E):
                out_copy(n, step, False).wait_send()

        for d in range(L):

            @pl.when((hi - d >= 0) & (hi + 1 <= top(n)))
            def _(n=n, d=d):
                line_copy(n, hi - d, True).wait_send()

            @pl.when((hi + d < L) & (hi - 1 >= bot(n)))
            def _(n=n, d=d):
                line_copy(n, hi + d, False).wait_send()


def on_device(nka, ncol, hamiltonian, eigvecs, spin, k_indices, r_vectors, degeneracy, fermi_level):
    WF = spin.shape[-1]
    L = nka // LO
    E = LO * ncol
    kdev = k_indices.shape[0]
    quarter = kdev // ncol
    rows = hamiltonian.shape[0] * 2
    nr = r_vectors.shape[0]
    width = WF * WF // E
    cw = math.lcm(WF, 128)
    nch = width // cw
    h = hamiltonian.reshape(rows, WF * WF)
    vm = pl.BlockSpec(memory_space=pltpu.VMEM)
    dma = pltpu.SemaphoreType.DMA
    cfg = (WF, L, ncol, rows, nch, cw, kdev, quarter, kdev * nka)
    blk = 8 * quarter
    curv, total = pl.pallas_call(
        functools.partial(kernel, cfg),
        name="spin_hall",
        out_shape=(
            jax.ShapeDtypeStruct((9, quarter, WF), f32),
            jax.ShapeDtypeStruct((9, WF), f32),
        ),
        in_specs=[vm] * 6 + [pl.BlockSpec(memory_space=pltpu.SMEM)],
        out_specs=(vm, vm),
        scratch_shapes=[
            pltpu.VMEM((8, 2 * nr), f32),
            pltpu.VMEM((2 * LO, kdev, PAD), f32),
            pltpu.VMEM((nch, nka * ncol, rows, cw), bf16),
            pltpu.VMEM((2 * E * blk, 2 * nr), bf16),
            pltpu.VMEM((nch, 2, E, blk, cw), bf16),
            pltpu.VMEM((nch, E, blk, cw), bf16),
            pltpu.VMEM((WF * 4 * quarter, PAD), f32),
            pltpu.VMEM((WF * 4 * quarter, PAD), f32),
            pltpu.VMEM((2, PAD, PAD), f32),
            pltpu.VMEM((5 * PAD, 2 * PAD), bf16),
            pltpu.VMEM((16, PAD), f32),
            pltpu.VMEM((E, 16, PAD), f32),
            pltpu.VMEM((L, 16, PAD), f32),
            dma((nch,)),
            dma((2, 4)),
            dma((nch, E)),
            dma((nch, E)),
            dma((nch, L, 2)),
            dma((nch, L)),
            dma((nch, 2, E)),
            dma((nch, E)),
            dma((E,)),
            dma((E,)),
            dma((L,)),
            dma((L,)),
        ],
        compiler_params=pltpu.CompilerParams(
            collective_id=0, has_side_effects=True, vmem_limit_bytes=60 * 1024 * 1024
        ),
    )(h, eigvecs, spin, k_indices.T, r_vectors.T, degeneracy.reshape(1, nr), fermi_level)
    return (jnp.transpose(curv, (0, 2, 1)), total)


def solution(mesh):
    in_specs = (
        P(("ka", "col"), None, None),
        P("ka", None, None, None),
        P(),
        P("ka", None),
        P(),
        P(),
        P(),
    )
    out_specs = (P(None, None, ("ka", "col")), P())
    body = functools.partial(on_device, mesh.shape["ka"], mesh.shape["col"])
    return jax.shard_map(body, mesh=mesh, in_specs=in_specs, out_specs=out_specs, check_vma=False)
```
